32 devices in a mesh: occ: 4 (over y, x), vir: 8 (over z, core).
Axes of the slice: x: 2, y: 2, z: 4, core: 2. Of those that a mesh axis runs over, the one named last changes fastest.
Arguments:
- amplitudes: bfloat16 [1504, 3072], P('occ', 'vir'), may hold values from -6 to 6
- integrals: bfloat16 [3072, 3072], P(None, 'vir'), may hold values from -0.15625 to 0.15625
- tile_block: int32 [24], replicated, may hold values from 0 to 5, as said below
- pair_mask: int32 [6, 6], replicated, may hold values 0 or 1
- partner: int32 [1504], P('occ'), may hold values from 0 to 1503, as said below
Outputs:
- residual: float32 [1504, 3072], P('occ', 'vir')
The draws below stay inside these ranges and needn't reach their ends.
Inputs may be any that keep to these rules, and one draw needn't show every extreme that they name: partner is an involution without fixed points: partner[partner[r]] = r and partner[r] != r. tile_block never falls along the tiles, and each of the 6 blocks holds at least one tile.
All inputs are finite; a program needn't handle non-finite values.
Results may differ from the reference program's by a relative error of at most 0.0003.
Values may be sent and summed in bfloat16 or wider, within the bound.
No kernel may reach another device: no remote copies, remote signals or barrier semaphores. Data moves between devices by JAX's collectives and lax.ppermute only.
A program may use at most 128 MiB of HBM per device.

```python
import jax
import jax.numpy as jnp
from jax import lax

TILE = 128
BLOCKS = 6
NIJ = 1504
NTILE = 24
VPAIRS = 3072


def draw_partner(key, part):
    shuffled = jax.random.permutation(jax.random.fold_in(key, 11), NIJ).astype(jnp.int32)
    swapped = shuffled.reshape(NIJ // 2, 2)[:, ::-1].reshape(NIJ)
    return jnp.zeros((NIJ,), jnp.int32).at[shuffled].set(swapped)


def draw_tile_block(key, part):
    order = jax.random.permutation(jax.random.fold_in(key, 23), NTILE - 1).astype(jnp.int32)
    cuts = order[:BLOCKS - 1] + 1
    tiles = jnp.arange(NTILE, dtype=jnp.int32)
    return jnp.sum((cuts[None, :] <= tiles[:, None]).astype(jnp.int32), axis=1).astype(jnp.int32)


def place_ends(array, stream_key, least, high):
    place = [jax.random.randint(jax.random.fold_in(stream_key, axis), (), 0, length) for axis, length in enumerate(array.shape)]
    longest = array.shape.index(max(array.shape))
    beside = place[:longest] + [(place[longest] + 1) % array.shape[longest]] + place[longest + 1:]
    return array.at[tuple(place)].set(least).at[tuple(beside)].set(high)


def levels(stream_key, extent, split, low, largest):
    factor_of = 1.0
    for position, parts in split:
        draws = jax.random.uniform(jax.random.fold_in(jax.random.fold_in(stream_key, 6), position), (parts,), jnp.float32, low / len(split), largest / len(split))
        factor_of = factor_of * jnp.repeat(jnp.exp(draws), extent[position] // parts).reshape((-1,) + (1,) * (len(extent) - 1 - position))
    return factor_of


def gaussian(stream_key, extent, width, most, shards=(), kind=jnp.bfloat16):
    values = jax.random.normal(stream_key, extent, jnp.float32) * width
    if len(shards) > 0:
        values = levels(stream_key, extent, shards, -0.22, 0.18) * values
    return jnp.clip(values, min=-most, max=most).astype(kind)


def setup_inputs(seed: int = 0) -> dict:
    keys = jax.random.split(jax.random.key(seed), 6)
    return {
        "amplitudes": gaussian(keys[0], (NIJ, VPAIRS), 1.0, 6.0, ((0, 4), (1, 8))),
        "integrals": gaussian(keys[1], (VPAIRS, VPAIRS), (VPAIRS // 2) ** -0.5, 0.15625, ((1, 8),)),
        "tile_block": draw_tile_block(jax.random.fold_in(keys[5], 71), 0),
        "pair_mask": place_ends((jax.random.randint(keys[3], (BLOCKS, BLOCKS), 0, 2) < 1).astype(jnp.int32), jax.random.fold_in(keys[3], 1), 0, 1),
        "partner": draw_partner(jax.random.fold_in(keys[5], 71), 0),
    }


def reference(amplitudes, integrals, tile_block, pair_mask, partner):
    def column(tile_index):
        strip_cols = lax.dynamic_slice_in_dim(integrals, tile_index * TILE, TILE, 1)
        live_tiles = pair_mask[tile_block, tile_block[tile_index]]
        row_mask = jnp.repeat(live_tiles, TILE).astype(jnp.bfloat16)
        return jnp.dot(amplitudes, strip_cols * row_mask[:, None], preferred_element_type=jnp.float32)

    blocks = lax.map(column, jnp.arange(NTILE, dtype=jnp.int32))
    ladder = jnp.transpose(blocks, (1, 0, 2)).reshape(NIJ, VPAIRS)
    return ladder - ladder[partner]
```

```python
import jax
import jax.numpy as jnp
from jax import lax
from jax.sharding import PartitionSpec as P

TILE = 128
SCALE = 4096.0


def split(values):
    wide = values.astype(jnp.float32)
    high = lax.reduce_precision(wide, 8, 7)
    return high.astype(jnp.bfloat16), (wide - high).astype(jnp.bfloat16)


def gather_line(own, planes):
    cores = 2
    near = [(p * cores + c, (p ^ 1) * cores + c) for p in range(planes) for c in range(cores)]
    middle = {0: 0, 1: 2, 2: 1, 3: 3}
    inner = [(p * cores + c, middle[p] * cores + c) for p in range(planes) for c in range(cores)]
    plane = lax.axis_index("vir") // cores
    is_inner = (plane == 1) | (plane == 2)
    first = lax.ppermute(own, "vir", near)
    across = lax.ppermute(own, "vir", inner)
    far_inner = lax.ppermute(first, "vir", inner)
    two_away = lax.ppermute(across, "vir", near)
    far_outer = lax.ppermute(far_inner, "vir", near)
    second = jnp.where(is_inner, far_inner, two_away)
    third = jnp.where(is_inner, across, far_outer)
    return [own, first, second, third]


def body(amplitudes, integrals, tile_block, pair_mask, partner, occ, vir):
    rows, width = amplitudes.shape
    columns = integrals.shape[1]
    local_tiles = columns // TILE
    total_tiles = tile_block.shape[0]
    groups = pair_mask.shape[0]
    here = lax.axis_index("vir")
    me = lax.axis_index("occ")

    received = [
        lax.ppermute(amplitudes, "occ", [(i, i ^ k) for i in range(occ)])
        for k in range(1, occ)
    ]
    slots = jnp.arange(rows, dtype=jnp.int32)

    def picked(block, source):
        onehot = (partner[:, None] == source * rows + slots[None, :]).astype(jnp.bfloat16)
        return jnp.dot(onehot, block, preferred_element_type=jnp.float32)

    difference = amplitudes.astype(jnp.float32) - picked(amplitudes, me)
    for k in range(1, occ):
        difference = difference - picked(received[k - 1], me ^ k)
    sent = (difference * SCALE).astype(jnp.float16)

    labels = jnp.arange(groups, dtype=jnp.int32)
    own_blocks = lax.dynamic_slice_in_dim(tile_block, here * local_tiles, local_tiles)
    row_onehot = (tile_block[:, None] == labels[None, :]).astype(jnp.float32)
    col_onehot = (own_blocks[:, None] == labels[None, :]).astype(jnp.float32)
    live = jnp.dot(jnp.dot(row_onehot, pair_mask.astype(jnp.float32)), col_onehot.T)
    live = jnp.repeat(live.astype(jnp.bfloat16), TILE, axis=1)
    masked = integrals.reshape(total_tiles, TILE, columns) * live[:, None, :]
    masked = masked.reshape(vir, width, columns)

    def product(piece, block):
        high, low = split(piece)
        rows_of_block = lax.dynamic_index_in_dim(masked, block, keepdims=False)
        return jnp.dot(high, rows_of_block, preferred_element_type=jnp.float32) + jnp.dot(
            low, rows_of_block, preferred_element_type=jnp.float32
        )

    if vir == 8:
        plane, core = here // 2, here % 2
        swap = [(i, i ^ 1) for i in range(vir)]
        total = jnp.zeros((rows, columns), jnp.float32)
        for step, item in enumerate(gather_line(sent, vir // 2)):
            total = total + product(item, (plane ^ step) * 2 + core)
            other = lax.ppermute(item, "vir", swap)
            total = total + product(other, (plane ^ step) * 2 + (core ^ 1))
    else:
        high, low = split(lax.all_gather(sent, "vir", axis=1, tiled=True))
        masked = masked.reshape(integrals.shape)
        total = jnp.dot(high, masked, preferred_element_type=jnp.float32)
        total = total + jnp.dot(low, masked, preferred_element_type=jnp.float32)
    return total * (1.0 / SCALE)


def solution(mesh):
    occ, vir = mesh.shape["occ"], mesh.shape["vir"]

    def whole(*args):
        return body(*args, occ, vir)

    placed = (P("occ", "vir"), P(None, "vir"), P(), P(), P("occ"))
    return jax.shard_map(
        whole, mesh=mesh, in_specs=placed, out_specs=P("occ", "vir"), check_vma=False
    )
```

```python
import functools

import jax
import jax.numpy as jnp
from jax import lax
from jax.experimental import pallas as pl
from jax.experimental.pallas import tpu as pltpu
from jax.sharding import PartitionSpec as P

TILE = 128
SCALE = 4096.0


def split(values):
    wide = values.astype(jnp.float32)
    high = lax.reduce_precision(wide, 8, 7)
    return high.astype(jnp.bfloat16), (wide - high).astype(jnp.bfloat16)


def trade(values, distance):
    return lax.ppermute(values, "vir", [(i, i ^ distance) for i in range(8)])


def contract_kernel(count, scale, order_ref, live_ref, *refs):
    pieces, refs = refs[: 2 * count], refs[2 * count :]
    base_ref = refs[0] if len(refs) == 5 else None
    integrals_ref, out_ref, block_ref, sems = refs[-4:]
    depth = block_ref.shape[1]
    tiles = depth // TILE
    copies = []
    for i in range(count):
        start = pl.multiple_of(order_ref[i] * depth, TILE)
        copies.append(
            pltpu.make_async_copy(
                integrals_ref.at[pl.ds(start, depth), :], block_ref.at[i], sems.at[i]
            )
        )
        copies[-1].start()
    total = None
    for i in range(count):
        copies[i].wait()
        rows = []
        for t in range(tiles):
            mask = live_ref[pl.ds(order_ref[i] * tiles + t, 1), :].astype(jnp.bfloat16)
            rows.append(block_ref[i, t * TILE : (t + 1) * TILE, :] * mask)
        block = jnp.concatenate(rows, axis=0)
        for part in pieces[2 * i : 2 * i + 2]:
            term = jnp.dot(part[...], block, preferred_element_type=jnp.float32)
            total = term if total is None else total + term
    if base_ref is not None:
        total = total + base_ref[...]
    out_ref[...] = total * scale if scale != 1.0 else total


def contract_body(items, order, live, integrals, base=None, scale=1.0):
    count = len(items)
    rows, depth = items[0].shape
    columns = integrals.shape[1]
    parts = [part for item in items for part in split(item)]
    extra = [] if base is None else [base]
    vmem = pl.BlockSpec(memory_space=pltpu.VMEM)
    flops = 4 * count * rows * depth * columns
    return pl.pallas_call(
        functools.partial(contract_kernel, count, scale),
        out_shape=jax.ShapeDtypeStruct((rows, columns), jnp.float32),
        in_specs=[pl.BlockSpec(memory_space=pltpu.SMEM), vmem]
        + [vmem] * (len(parts) + len(extra))
        + [pl.BlockSpec(memory_space=pl.ANY)],
        out_specs=vmem,
        scratch_shapes=[
            pltpu.VMEM((count, depth, columns), jnp.bfloat16),
            pltpu.SemaphoreType.DMA((count,)),
        ],
        compiler_params=pltpu.CompilerParams(vmem_limit_bytes=12 << 20),
        cost_estimate=pl.CostEstimate(
            flops=flops, transcendentals=0, bytes_accessed=2 * count * depth * columns
        ),
    )(jnp.stack(order).astype(jnp.int32), live, *parts, *extra, integrals)


def body(amplitudes, integrals, tile_block, pair_mask, partner, occ, vir):
    rows, _ = amplitudes.shape
    columns = integrals.shape[1]
    local_tiles = columns // TILE
    total_tiles = tile_block.shape[0]
    groups = pair_mask.shape[0]
    here = lax.axis_index("vir")
    me = lax.axis_index("occ")

    slots = jnp.arange(rows, dtype=jnp.int32)

    def picked(block, source):
        onehot = (partner[:, None] == source * rows + slots[None, :]).astype(jnp.bfloat16)
        return jnp.dot(onehot, block, preferred_element_type=jnp.float32)

    received = [
        lax.ppermute(amplitudes, "occ", [(i, i ^ k) for i in range(occ)]) for k in range(1, occ)
    ]
    difference = amplitudes.astype(jnp.float32) - picked(amplitudes, me)
    for k in range(1, occ):
        difference = difference - picked(received[k - 1], me ^ k)
    own = (difference * SCALE).astype(jnp.float16)

    labels = jnp.arange(groups, dtype=jnp.int32)
    own_blocks = lax.dynamic_slice_in_dim(tile_block, here * local_tiles, local_tiles)
    row_onehot = (tile_block[:, None] == labels[None, :]).astype(jnp.float32)
    col_onehot = (own_blocks[:, None] == labels[None, :]).astype(jnp.float32)
    live = jnp.dot(jnp.dot(row_onehot, pair_mask.astype(jnp.float32)), col_onehot.T)
    live = jnp.repeat(live, TILE, axis=1)

    if vir != 8:
        masked = integrals.reshape(total_tiles, TILE, columns)
        masked = masked * live.astype(jnp.bfloat16)[:, None, :]
        masked = masked.reshape(integrals.shape)
        high, low = split(lax.all_gather(own, "vir", axis=1, tiled=True))
        total = jnp.dot(high, masked, preferred_element_type=jnp.float32)
        total = total + jnp.dot(low, masked, preferred_element_type=jnp.float32)
        return total * (1.0 / SCALE)

    plane, core = here // 2, here % 2

    def place(step, other):
        return (plane ^ step) * 2 + (core ^ other)

    own = lax.optimization_barrier(own)
    third = trade(own, 6)
    first = trade(own, 2)
    second = trade(third, 2)
    total = contract_body(
        [own, trade(own, 1)], [place(0, 0), place(0, 1)], live, integrals
    )
    total = contract_body(
        [first, trade(first, 1), third, trade(third, 1)],
        [place(1, 0), place(1, 1), place(3, 0), place(3, 1)],
        live,
        integrals,
        total,
    )
    total = contract_body([second], [place(2, 0)], live, integrals, total)
    return contract_body(
        [trade(second, 1)], [place(2, 1)], live, integrals, total, 1.0 / SCALE
    )


def solution(mesh):
    occ, vir = mesh.shape["occ"], mesh.shape["vir"]

    def whole(*args):
        return body(*args, occ, vir)

    placed = (P("occ", "vir"), P(None, "vir"), P(), P(), P("occ"))
    return jax.shard_map(
        whole, mesh=mesh, in_specs=placed, out_specs=P("occ", "vir"), check_vma=False
    )
```

```python
import functools

import jax
import jax.numpy as jnp
from jax import lax
from jax.experimental import pallas as pl
from jax.experimental.pallas import tpu as pltpu
from jax.sharding import PartitionSpec as P

TILE = 128
SCALE = 4096.0
CHUNKS = (2, 1)


def split(values):
    wide = values.astype(jnp.float32)
    high = lax.reduce_precision(wide, 8, 7)
    return high.astype(jnp.bfloat16), (wide - high).astype(jnp.bfloat16)


def trade(values, distance):
    return lax.ppermute(values, "vir", [(i, i ^ distance) for i in range(8)])


def cut_kernel(spans, source_ref, *refs):
    pieces, sems = refs[:-1], refs[-1]
    copies = []
    for i, (start, stop) in enumerate(spans):
        copies.append(
            pltpu.make_async_copy(source_ref.at[:, start:stop], pieces[i], sems.at[i])
        )
        copies[-1].start()
    for copy in copies:
        copy.wait()


def cut(source, spans):
    rows = source.shape[0]
    return pl.pallas_call(
        functools.partial(cut_kernel, spans),
        out_shape=[jax.ShapeDtypeStruct((rows, b - a), source.dtype) for a, b in spans],
        in_specs=[pl.BlockSpec(memory_space=pl.ANY)],
        out_specs=[pl.BlockSpec(memory_space=pltpu.VMEM)] * len(spans),
        scratch_shapes=[pltpu.SemaphoreType.DMA((len(spans),))],
        compiler_params=pltpu.CompilerParams(vmem_limit_bytes=4 << 20),
    )(source)


def masked_rows(block_ref, live_ref, first, at, depth):
    rows = []
    for t in range(depth // TILE):
        mask = live_ref[pl.ds(first + t, 1), :].astype(jnp.bfloat16)
        rows.append(block_ref[at + t * TILE : at + (t + 1) * TILE, :] * mask)
    return jnp.concatenate(rows, axis=0)


def contract_kernel(depths, ahead, has_base, origin_ref, live_ref, *refs):
    count = len(depths)
    pieces, refs = refs[: 2 * count], refs[2 * count :]
    if has_base:
        base_ref, refs = refs[0], refs[1:]
    integrals_ref, out_ref = refs[:2]
    kept, (block_ref, sems) = refs[2:-2], refs[-2:]
    copies, at = [], [0]
    for i, depth in enumerate(depths + ahead):
        start = pl.multiple_of(origin_ref[i] * TILE, TILE)
        copies.append(
            pltpu.make_async_copy(
                integrals_ref.at[pl.ds(start, depth), :],
                block_ref.at[pl.ds(at[-1], depth), :],
                sems.at[i],
            )
        )
        copies[-1].start()
        at.append(at[-1] + depth)
    total = base_ref[...] if has_base else None
    for i, depth in enumerate(depths):
        copies[i].wait()
        block = masked_rows(block_ref, live_ref, origin_ref[i], at[i], depth)
        for part in pieces[2 * i : 2 * i + 2]:
            term = jnp.dot(part[...], block, preferred_element_type=jnp.float32)
            total = term if total is None else total + term
    out_ref[...] = total
    for i, depth in enumerate(ahead):
        copies[count + i].wait()
        kept[i][...] = masked_rows(
            block_ref, live_ref, origin_ref[count + i], at[count + i], depth
        )


def contract(items, live, integrals, base=None, ahead=()):
    rows = items[0][0].shape[0]
    columns = integrals.shape[1]
    depths = tuple(item.shape[1] for item, _ in items)
    later = tuple(depth for _, depth in ahead)
    parts = [part for item, _ in items for part in split(item)]
    extra = [] if base is None else [base]
    tiles = [tile for _, tile in items] + [tile for tile, _ in ahead]
    vmem = pl.BlockSpec(memory_space=pltpu.VMEM)
    depth = sum(depths + later)
    return pl.pallas_call(
        functools.partial(contract_kernel, depths, later, base is not None),
        out_shape=[jax.ShapeDtypeStruct((rows, columns), jnp.float32)]
        + [jax.ShapeDtypeStruct((d, columns), jnp.bfloat16) for d in later],
        in_specs=[pl.BlockSpec(memory_space=pltpu.SMEM), vmem]
        + [vmem] * (len(parts) + len(extra))
        + [pl.BlockSpec(memory_space=pltpu.HBM)],
        out_specs=[vmem] * (1 + len(later)),
        scratch_shapes=[
            pltpu.VMEM((depth, columns), jnp.bfloat16),
            pltpu.SemaphoreType.DMA((len(tiles),)),
        ],
        compiler_params=pltpu.CompilerParams(vmem_limit_bytes=14 << 20),
        cost_estimate=pl.CostEstimate(
            flops=4 * rows * columns * sum(depths),
            transcendentals=0,
            bytes_accessed=2 * depth * columns,
        ),
    )(
        jnp.stack(tiles).astype(jnp.int32),
        live,
        *parts,
        *extra,
        pltpu.with_memory_space_constraint(integrals, pltpu.HBM),
    )


def finish_kernel(count, scale, *refs):
    pieces, blocks, base_ref, out_ref = refs[: 2 * count], refs[2 * count : -2], refs[-2], refs[-1]
    total = base_ref[...]
    for i in range(count):
        for part in pieces[2 * i : 2 * i + 2]:
            total = total + jnp.dot(
                part[...], blocks[i][...], preferred_element_type=jnp.float32
            )
    out_ref[...] = total if scale == 1.0 else total * scale


def finish(items, blocks, base, scale=1.0):
    parts = [part for item in items for part in split(item)]
    vmem = pl.BlockSpec(memory_space=pltpu.VMEM)
    return pl.pallas_call(
        functools.partial(finish_kernel, len(items), scale),
        out_shape=jax.ShapeDtypeStruct(base.shape, jnp.float32),
        in_specs=[vmem] * (len(parts) + len(blocks) + 1),
        out_specs=vmem,
        compiler_params=pltpu.CompilerParams(vmem_limit_bytes=14 << 20),
        cost_estimate=pl.CostEstimate(
            flops=4 * base.size * sum(item.shape[1] for item in items),
            transcendentals=0,
            bytes_accessed=4 * base.size,
        ),
    )(*parts, *blocks, base)


def body(amplitudes, integrals, tile_block, pair_mask, partner, occ, vir):
    rows, width = amplitudes.shape
    columns = integrals.shape[1]
    local_tiles = columns // TILE
    total_tiles = tile_block.shape[0]
    groups = pair_mask.shape[0]
    here = lax.axis_index("vir")
    me = lax.axis_index("occ")

    spans, at = [], 0
    for share in CHUNKS:
        spans.append((at, at + width * share // sum(CHUNKS)))
        at = spans[-1][1]
    chunks = range(len(spans))

    slots = jnp.arange(rows, dtype=jnp.int32)

    def chosen(source):
        onehot = (partner[:, None] == source * rows + slots[None, :]).astype(jnp.bfloat16)
        return lax.optimization_barrier(onehot)

    select = [chosen(me ^ hop) for hop in range(occ)]

    def picked(block, hop):
        return jnp.dot(select[hop], block, preferred_element_type=jnp.float32)

    pieces = list(cut(amplitudes, spans))
    differences, received = [], []
    for k in chunks:
        received.append(
            [
                lax.ppermute(pieces[k], "occ", [(i, i ^ hop) for i in range(occ)])
                for hop in range(1, occ)
            ]
        )
        differences.append(pieces[k].astype(jnp.float32) - picked(pieces[k], 0))
    sent = []
    for k, difference in enumerate(differences):
        for hop in range(1, occ):
            difference = difference - picked(received[k][hop - 1], hop)
        sent.append((difference * SCALE).astype(jnp.float16))

    labels = jnp.arange(groups, dtype=jnp.int32)
    own_blocks = lax.dynamic_slice_in_dim(tile_block, here * local_tiles, local_tiles)
    row_onehot = (tile_block[:, None] == labels[None, :]).astype(jnp.float32)
    col_onehot = (own_blocks[:, None] == labels[None, :]).astype(jnp.float32)
    live = jnp.dot(jnp.dot(row_onehot, pair_mask.astype(jnp.float32)), col_onehot.T)
    live = jnp.repeat(live, TILE, axis=1)

    if vir != 8:
        masked = integrals.reshape(total_tiles, TILE, columns)
        masked = masked * live.astype(jnp.bfloat16)[:, None, :]
        masked = masked.reshape(integrals.shape)
        whole = lax.all_gather(jnp.concatenate(sent, axis=1), "vir", axis=1, tiled=True)
        high, low = split(whole)
        total = jnp.dot(high, masked, preferred_element_type=jnp.float32)
        total = total + jnp.dot(low, masked, preferred_element_type=jnp.float32)
        return total * (1.0 / SCALE)

    plane, core = here // 2, here % 2

    def tile_of(k, step, other):
        shard = (plane ^ step) * 2 + (core ^ other)
        return shard * (width // TILE) + spans[k][0] // TILE

    def pair(k, item, step):
        return [
            (item, tile_of(k, step, 0)),
            (trade(item, 1), tile_of(k, step, 1)),
        ]

    own = [lax.optimization_barrier(item) for item in sent]
    third = [trade(own[k], 6) for k in chunks]
    first = [trade(own[k], 2) for k in chunks]
    second = [trade(third[k], 2) for k in chunks]

    early = [x for k in chunks for x in pair(k, own[k], 0)]
    middle = [x for k in chunks for x in pair(k, third[k], 3)]
    middle += [x for k in chunks for x in pair(k, first[k], 1)]
    late = [x for k in chunks for x in pair(k, second[k], 2)]
    ahead = [(tile, item.shape[1]) for item, tile in late]
    items = [item for item, _ in late]
    (total,) = contract(early, live, integrals)
    total, *blocks = contract(middle, live, integrals, total, ahead)
    total = finish(items[:-1], blocks[:-1], total)
    return finish(items[-1:], blocks[-1:], total, 1.0 / SCALE)


def solution(mesh):
    occ, vir = mesh.shape["occ"], mesh.shape["vir"]

    def whole(*args):
        return body(*args, occ, vir)

    placed = (P("occ", "vir"), P(None, "vir"), P(), P(), P("occ"))
    return jax.shard_map(
        whole, mesh=mesh, in_specs=placed, out_specs=P("occ", "vir"), check_vma=False
    )
```

```python
import functools

import jax
import jax.numpy as jnp
from jax import lax
from jax.experimental import pallas as pl
from jax.experimental.pallas import tpu as pltpu
from jax.sharding import PartitionSpec as P

TILE = 128
SCALE = 4096.0
CHUNKS = (2, 1)
INPLACE = True
STEPS = 3


def split(values):
    wide = values.astype(jnp.float32)
    high = lax.reduce_precision(wide, 8, 7)
    return high.astype(jnp.bfloat16), (wide - high).astype(jnp.bfloat16)


def trade(values, distance):
    return lax.ppermute(values, "vir", [(i, i ^ distance) for i in range(8)])


def cut_kernel(spans, source_ref, *refs):
    pieces, sems = refs[:-1], refs[-1]
    copies = []
    for i, (start, stop) in enumerate(spans):
        copies.append(
            pltpu.make_async_copy(source_ref.at[:, start:stop], pieces[i], sems.at[i])
        )
        copies[-1].start()
    for copy in copies:
        copy.wait()


def cut(source, spans):
    rows = source.shape[0]
    return pl.pallas_call(
        functools.partial(cut_kernel, spans),
        out_shape=[jax.ShapeDtypeStruct((rows, b - a), source.dtype) for a, b in spans],
        in_specs=[pl.BlockSpec(memory_space=pl.ANY)],
        out_specs=[pl.BlockSpec(memory_space=pltpu.VMEM)] * len(spans),
        scratch_shapes=[pltpu.SemaphoreType.DMA((len(spans),))],
        compiler_params=pltpu.CompilerParams(vmem_limit_bytes=4 << 20),
    )(source)


def contract_kernel(depths, ahead, inner, has_base, scale, *refs):
    count, later = len(depths), len(ahead)
    if later:
        (origin_ref, live_ref, integrals_ref), refs = refs[:3], refs[3:]
        (block_ref, sems), refs = refs[-2:], refs[:-2]
    pieces, refs = refs[: 2 * count], refs[2 * count :]
    ready = count - inner
    blocks, refs = refs[:ready], refs[ready:]
    if has_base:
        base_ref, refs = refs[0], refs[1:]
    copies, at = [], [0]
    for i, depth in enumerate(ahead):
        start = pl.multiple_of(origin_ref[i] * TILE, TILE)
        copies.append(
            pltpu.make_async_copy(
                integrals_ref.at[pl.ds(start, depth), :],
                block_ref.at[pl.ds(at[-1], depth), :],
                sems.at[i],
            )
        )
        copies[-1].start()
        at.append(at[-1] + depth)

    def masked(i):
        copies[i].wait()
        rows = []
        for t in range(ahead[i] // TILE):
            mask = live_ref[pl.ds(origin_ref[i] + t, 1), :].astype(jnp.bfloat16)
            rows.append(block_ref[at[i] + t * TILE : at[i] + (t + 1) * TILE, :] * mask)
        return rows

    if count:
        total = base_ref[...] if has_base else None
        for i in range(count):
            block = blocks[i][...] if i < ready else jnp.concatenate(masked(i - ready))
            for part in pieces[2 * i : 2 * i + 2]:
                term = jnp.dot(part[...], block, preferred_element_type=jnp.float32)
                total = term if total is None else total + term
        refs[0][...] = total if scale == 1.0 else total * scale
        refs = refs[1:]
    for i in range(inner, later):
        for t, rows in enumerate(masked(i)):
            refs[i - inner][t * TILE : (t + 1) * TILE, :] = rows


def contract(shape, items, blocks, base=None, scale=1.0, ahead=(), source=None):
    rows, columns = shape
    depths = tuple(item.shape[1] for item in items)
    later = tuple(depth for _, depth in ahead)
    inner = len(items) - len(blocks) if items else 0
    vmem = pl.BlockSpec(memory_space=pltpu.VMEM)
    args, specs, out, scratch = [], [], [], []
    if ahead:
        live, integrals = source
        args = [
            jnp.stack([tile for tile, _ in ahead]).astype(jnp.int32),
            live,
            pltpu.with_memory_space_constraint(integrals, pltpu.HBM),
        ]
        specs = [pl.BlockSpec(memory_space=pltpu.SMEM), vmem, pl.BlockSpec(memory_space=pltpu.HBM)]
        scratch = [
            pltpu.VMEM((sum(later), columns), jnp.bfloat16),
            pltpu.SemaphoreType.DMA((len(later),)),
        ]
    args += [part for item in items for part in split(item)] + list(blocks)
    alias = {}
    if base is not None:
        if INPLACE and scale == 1.0:
            alias = {len(args): 0}
        args.append(base)
    specs += [vmem] * (len(args) - len(specs))
    if items:
        out.append(jax.ShapeDtypeStruct((rows, columns), jnp.float32))
    out += [jax.ShapeDtypeStruct((depth, columns), jnp.bfloat16) for depth in later[inner:]]
    return pl.pallas_call(
        functools.partial(contract_kernel, depths, later, inner, base is not None, scale),
        out_shape=out,
        in_specs=specs,
        out_specs=[vmem] * len(out),
        scratch_shapes=scratch,
        input_output_aliases=alias,
        compiler_params=pltpu.CompilerParams(vmem_limit_bytes=10 << 20),
        cost_estimate=pl.CostEstimate(
            flops=4 * rows * columns * sum(depths),
            transcendentals=0,
            bytes_accessed=8 * rows * columns,
        ),
    )(*args)


def finish_kernel(count, steps, *refs):
    pieces, blocks = refs[: 2 * count], refs[2 * count : 3 * count]
    base_ref, out_ref, sum_ref, sems = refs[3 * count :]
    copies = []
    for i, (start, stop) in enumerate(steps):
        rows = slice(start, stop)
        total = base_ref[rows, :]
        for j in range(count):
            for part in pieces[2 * j : 2 * j + 2]:
                total = total + jnp.dot(
                    part[rows, :], blocks[j][...], preferred_element_type=jnp.float32
                )
        sum_ref[rows, :] = total * (1.0 / SCALE)
        copies.append(pltpu.make_async_copy(sum_ref.at[rows, :], out_ref.at[rows, :], sems.at[i]))
        copies[-1].start()
    for copy in copies:
        copy.wait()


def finish(items, blocks, base):
    rows, columns = base.shape
    size = -(-rows // (8 * STEPS)) * 8
    steps = [(a, min(a + size, rows)) for a in range(0, rows, size)]
    vmem = pl.BlockSpec(memory_space=pltpu.VMEM)
    parts = [part for item in items for part in split(item)]
    return pl.pallas_call(
        functools.partial(finish_kernel, len(items), steps),
        out_shape=jax.ShapeDtypeStruct((rows, columns), jnp.float32),
        in_specs=[vmem] * (len(parts) + len(blocks) + 1),
        out_specs=pl.BlockSpec(memory_space=pltpu.HBM),
        scratch_shapes=[
            pltpu.VMEM((rows, columns), jnp.float32),
            pltpu.SemaphoreType.DMA((len(steps),)),
        ],
        compiler_params=pltpu.CompilerParams(vmem_limit_bytes=10 << 20),
    )(*parts, *blocks, base)


def body(amplitudes, integrals, tile_block, pair_mask, partner, occ, vir):
    rows, width = amplitudes.shape
    columns = integrals.shape[1]
    local_tiles = columns // TILE
    total_tiles = tile_block.shape[0]
    groups = pair_mask.shape[0]
    here = lax.axis_index("vir")
    me = lax.axis_index("occ")

    spans, at = [], 0
    for share in CHUNKS:
        spans.append((at, at + width * share // sum(CHUNKS)))
        at = spans[-1][1]
    chunks = range(len(spans))

    slots = jnp.arange(rows, dtype=jnp.int32)

    def chosen(source):
        onehot = (partner[:, None] == source * rows + slots[None, :]).astype(jnp.bfloat16)
        return lax.optimization_barrier(onehot)

    select = [chosen(me ^ hop) for hop in range(occ)]

    def picked(block, hop):
        return jnp.dot(select[hop], block, preferred_element_type=jnp.float32)

    pieces = list(cut(amplitudes, spans))
    differences, received = [], []
    for k in chunks:
        received.append(
            [
                lax.ppermute(pieces[k], "occ", [(i, i ^ hop) for i in range(occ)])
                for hop in range(1, occ)
            ]
        )
        differences.append(pieces[k].astype(jnp.float32) - picked(pieces[k], 0))
    sent = []
    for k, difference in enumerate(differences):
        for hop in range(1, occ):
            difference = difference - picked(received[k][hop - 1], hop)
        sent.append((difference * SCALE).astype(jnp.float16))

    labels = jnp.arange(groups, dtype=jnp.int32)
    own_blocks = lax.dynamic_slice_in_dim(tile_block, here * local_tiles, local_tiles)
    row_onehot = (tile_block[:, None] == labels[None, :]).astype(jnp.float32)
    col_onehot = (own_blocks[:, None] == labels[None, :]).astype(jnp.float32)
    live = jnp.dot(jnp.dot(row_onehot, pair_mask.astype(jnp.float32)), col_onehot.T)
    live = jnp.repeat(live, TILE, axis=1)

    if vir != 8:
        masked = integrals.reshape(total_tiles, TILE, columns)
        masked = masked * live.astype(jnp.bfloat16)[:, None, :]
        masked = masked.reshape(integrals.shape)
        whole = lax.all_gather(jnp.concatenate(sent, axis=1), "vir", axis=1, tiled=True)
        high, low = split(whole)
        total = jnp.dot(high, masked, preferred_element_type=jnp.float32)
        total = total + jnp.dot(low, masked, preferred_element_type=jnp.float32)
        return total * (1.0 / SCALE)

    plane, core = here // 2, here % 2

    def rows_for(step, start, depth):
        return [
            (((plane ^ step) * 2 + (core ^ c)) * (width // TILE) + start // TILE, depth)
            for c in (0, 1)
        ]

    def pair(item):
        return [item, trade(item, 1)]

    own = [lax.optimization_barrier(item) for item in sent]
    whole = jnp.concatenate(own, axis=1)
    third = [trade(own[k], 6) for k in chunks]
    first = [trade(own[k], 2) for k in chunks]
    second = [trade(third[k], 2) for k in chunks]

    shape, source = (rows, columns), (live, integrals)
    parts = [(a, b - a) for a, b in spans]
    for_middle = [x for step in (3, 1) for part in parts for x in rows_for(step, *part)]
    for_late = [rows_for(2, *part)[c] for c in (0, 1) for part in parts]
    blocks = contract(shape, [], [], ahead=rows_for(0, 0, width)[:1], source=source)
    total, *blocks = contract(
        shape, pair(whole), blocks, ahead=rows_for(0, 0, width)[1:] + for_middle, source=source
    )
    items = [x for k in chunks for x in pair(third[k])]
    items += [x for k in chunks for x in pair(first[k])]
    total, *blocks = contract(shape, items, blocks, total, ahead=for_late, source=source)
    count = len(chunks)
    swapped = [trade(second[k], 1) for k in chunks]
    (total,) = contract(shape, second, blocks[:count], total)
    return finish(swapped, blocks[count:], total)


def solution(mesh):
    occ, vir = mesh.shape["occ"], mesh.shape["vir"]

    def whole(*args):
        return body(*args, occ, vir)

    placed = (P("occ", "vir"), P(None, "vir"), P(), P(), P("occ"))
    return jax.shard_map(
        whole, mesh=mesh, in_specs=placed, out_specs=P("occ", "vir"), check_vma=False
    )
```

```python
import functools

import jax
import jax.numpy as jnp
from jax import lax
from jax.experimental import pallas as pl
from jax.experimental.pallas import tpu as pltpu
from jax.sharding import PartitionSpec as P

TILE = 128
SCALE = 4096.0
CHUNKS = (2, 1)
INPLACE = True
STEPS = 6


def split(values):
    wide = values.astype(jnp.float32)
    high = lax.reduce_precision(wide, 8, 7)
    return high.astype(jnp.bfloat16), (wide - high).astype(jnp.bfloat16)


def trade(values, distance):
    return lax.ppermute(values, "vir", [(i, i ^ distance) for i in range(8)])


def cut_kernel(spans, source_ref, *refs):
    pieces, sems = refs[:-1], refs[-1]
    copies = []
    for i, (start, stop) in enumerate(spans):
        copies.append(
            pltpu.make_async_copy(source_ref.at[:, start:stop], pieces[i], sems.at[i])
        )
        copies[-1].start()
    for copy in copies:
        copy.wait()


def cut(source, spans):
    rows = source.shape[0]
    return pl.pallas_call(
        functools.partial(cut_kernel, spans),
        out_shape=[jax.ShapeDtypeStruct((rows, b - a), source.dtype) for a, b in spans],
        in_specs=[pl.BlockSpec(memory_space=pl.ANY)],
        out_specs=[pl.BlockSpec(memory_space=pltpu.VMEM)] * len(spans),
        scratch_shapes=[pltpu.SemaphoreType.DMA((len(spans),))],
        compiler_params=pltpu.CompilerParams(vmem_limit_bytes=4 << 20),
    )(source)


def contract_kernel(depths, ahead, has_base, scale, *refs):
    count, later = len(depths), len(ahead)
    if later:
        (origin_ref, live_ref, integrals_ref), refs = refs[:3], refs[3:]
        (block_ref, sems), refs = refs[-2:], refs[:-2]
    pieces, refs = refs[: 2 * count], refs[2 * count :]
    blocks, refs = refs[:count], refs[count:]
    if has_base:
        base_ref, refs = refs[0], refs[1:]
    copies, at = [], [0]
    for i, depth in enumerate(ahead):
        start = pl.multiple_of(origin_ref[i] * TILE, TILE)
        copies.append(
            pltpu.make_async_copy(
                integrals_ref.at[pl.ds(start, depth), :],
                block_ref.at[pl.ds(at[-1], depth), :],
                sems.at[i],
            )
        )
        copies[-1].start()
        at.append(at[-1] + depth)
    if count:
        total = base_ref[...] if has_base else None
        for i in range(count):
            block = blocks[i][...]
            for part in pieces[2 * i : 2 * i + 2]:
                term = jnp.dot(part[...], block, preferred_element_type=jnp.float32)
                total = term if total is None else total + term
        refs[0][...] = total if scale == 1.0 else total * scale
        refs = refs[1:]
    for i, depth in enumerate(ahead):
        copies[i].wait()
        for t in range(depth // TILE):
            mask = live_ref[pl.ds(origin_ref[i] + t, 1), :].astype(jnp.bfloat16)
            rows = slice(at[i] + t * TILE, at[i] + (t + 1) * TILE)
            refs[i][t * TILE : (t + 1) * TILE, :] = block_ref[rows, :] * mask


def contract(shape, items, blocks, base=None, scale=1.0, ahead=(), source=None):
    rows, columns = shape
    depths = tuple(item.shape[1] for item in items)
    later = tuple(depth for _, depth in ahead)
    vmem = pl.BlockSpec(memory_space=pltpu.VMEM)
    args, specs, out, scratch = [], [], [], []
    if ahead:
        live, integrals = source
        args = [
            jnp.stack([tile for tile, _ in ahead]).astype(jnp.int32),
            live,
            pltpu.with_memory_space_constraint(integrals, pltpu.HBM),
        ]
        specs = [
            pl.BlockSpec(memory_space=pltpu.SMEM),
            vmem,
            pl.BlockSpec(memory_space=pltpu.HBM),
        ]
        scratch = [
            pltpu.VMEM((sum(later), columns), jnp.bfloat16),
            pltpu.SemaphoreType.DMA((len(later),)),
        ]
    args += [part for item in items for part in split(item)] + list(blocks)
    alias = {}
    if base is not None:
        if INPLACE and scale == 1.0:
            alias = {len(args): 0}
        args.append(base)
    specs += [vmem] * (len(args) - len(specs))
    if items:
        out.append(jax.ShapeDtypeStruct((rows, columns), jnp.float32))
    out += [jax.ShapeDtypeStruct((depth, columns), jnp.bfloat16) for depth in later]
    return pl.pallas_call(
        functools.partial(contract_kernel, depths, later, base is not None, scale),
        out_shape=out,
        in_specs=specs,
        out_specs=[vmem] * len(out),
        scratch_shapes=scratch,
        input_output_aliases=alias,
        compiler_params=pltpu.CompilerParams(vmem_limit_bytes=10 << 20),
        cost_estimate=pl.CostEstimate(
            flops=4 * rows * columns * sum(depths),
            transcendentals=0,
            bytes_accessed=8 * rows * columns,
        ),
    )(*args)


def finish_kernel(count, steps, *refs):
    pieces, blocks = refs[: 2 * count], refs[2 * count : 3 * count]
    base_ref, out_ref, sum_ref, sems = refs[3 * count :]
    copies = []
    for i, (start, stop) in enumerate(steps):
        rows = slice(start, stop)
        total = base_ref[rows, :]
        for j in range(count):
            for part in pieces[2 * j : 2 * j + 2]:
                total = total + jnp.dot(
                    part[rows, :], blocks[j][...], preferred_element_type=jnp.float32
                )
        sum_ref[rows, :] = total * (1.0 / SCALE)
        copies.append(pltpu.make_async_copy(sum_ref.at[rows, :], out_ref.at[rows, :], sems.at[i]))
        copies[-1].start()
    for copy in copies:
        copy.wait()


def finish(items, blocks, base):
    rows, columns = base.shape
    size = -(-rows // (8 * STEPS)) * 8
    steps = [(a, min(a + size, rows)) for a in range(0, rows, size)]
    vmem = pl.BlockSpec(memory_space=pltpu.VMEM)
    parts = [part for item in items for part in split(item)]
    return pl.pallas_call(
        functools.partial(finish_kernel, len(items), steps),
        out_shape=jax.ShapeDtypeStruct((rows, columns), jnp.float32),
        in_specs=[vmem] * (len(parts) + len(blocks) + 1),
        out_specs=pl.BlockSpec(memory_space=pltpu.HBM),
        scratch_shapes=[
            pltpu.VMEM((rows, columns), jnp.float32),
            pltpu.SemaphoreType.DMA((len(steps),)),
        ],
        compiler_params=pltpu.CompilerParams(vmem_limit_bytes=10 << 20),
    )(*parts, *blocks, base)


def body(amplitudes, integrals, tile_block, pair_mask, partner, occ, vir):
    rows, width = amplitudes.shape
    columns = integrals.shape[1]
    local_tiles = columns // TILE
    total_tiles = tile_block.shape[0]
    groups = pair_mask.shape[0]
    here = lax.axis_index("vir")
    me = lax.axis_index("occ")

    spans, at = [], 0
    for share in CHUNKS:
        spans.append((at, at + width * share // sum(CHUNKS)))
        at = spans[-1][1]
    chunks = range(len(spans))

    slots = jnp.arange(rows, dtype=jnp.int32)

    def chosen(source):
        onehot = (partner[:, None] == source * rows + slots[None, :]).astype(jnp.bfloat16)
        return lax.optimization_barrier(onehot)

    select = [chosen(me ^ hop) for hop in range(occ)]

    def picked(block, hop):
        return jnp.dot(select[hop], block, preferred_element_type=jnp.float32)

    pieces = list(cut(amplitudes, spans))
    differences, received = [], []
    for k in chunks:
        received.append(
            [
                lax.ppermute(pieces[k], "occ", [(i, i ^ hop) for i in range(occ)])
                for hop in range(1, occ)
            ]
        )
        differences.append(pieces[k].astype(jnp.float32) - picked(pieces[k], 0))
    sent = []
    for k, difference in enumerate(differences):
        for hop in range(1, occ):
            difference = difference - picked(received[k][hop - 1], hop)
        sent.append((difference * SCALE).astype(jnp.float16))

    labels = jnp.arange(groups, dtype=jnp.int32)
    own_blocks = lax.dynamic_slice_in_dim(tile_block, here * local_tiles, local_tiles)
    row_onehot = (tile_block[:, None] == labels[None, :]).astype(jnp.float32)
    col_onehot = (own_blocks[:, None] == labels[None, :]).astype(jnp.float32)
    live = jnp.dot(jnp.dot(row_onehot, pair_mask.astype(jnp.float32)), col_onehot.T)
    live = jnp.repeat(live, TILE, axis=1)

    if vir != 8:
        masked = integrals.reshape(total_tiles, TILE, columns)
        masked = masked * live.astype(jnp.bfloat16)[:, None, :]
        masked = masked.reshape(integrals.shape)
        whole = lax.all_gather(jnp.concatenate(sent, axis=1), "vir", axis=1, tiled=True)
        high, low = split(whole)
        total = jnp.dot(high, masked, preferred_element_type=jnp.float32)
        total = total + jnp.dot(low, masked, preferred_element_type=jnp.float32)
        return total * (1.0 / SCALE)

    plane, core = here // 2, here % 2

    def rows_for(step, start, depth):
        return [
            (((plane ^ step) * 2 + (core ^ c)) * (width // TILE) + start // TILE, depth)
            for c in (0, 1)
        ]

    def pair(item):
        return [item, trade(item, 1)]

    own = [lax.optimization_barrier(item) for item in sent]
    whole = jnp.concatenate(own, axis=1)
    third = [trade(own[k], 6) for k in chunks]
    first = [trade(own[k], 2) for k in chunks]
    second = [trade(third[k], 2) for k in chunks]

    shape, source = (rows, columns), (live, integrals)
    parts = [(a, b - a) for a, b in spans]
    for_middle = [x for step in (3, 1) for part in parts for x in rows_for(step, *part)]
    for_late = [rows_for(2, *part)[c] for c in (0, 1) for part in parts]
    blocks = contract(shape, [], [], ahead=rows_for(0, 0, width), source=source)
    total, *blocks = contract(
        shape, pair(whole), blocks, ahead=for_middle, source=source
    )
    items = [x for k in chunks for x in pair(third[k])]
    items += [x for k in chunks for x in pair(first[k])]
    total, *blocks = contract(
        shape, items, blocks, total, ahead=for_late, source=source
    )
    count = len(chunks)
    swapped = [trade(second[k], 1) for k in chunks]
    (total,) = contract(shape, second, blocks[:count], total)
    return finish(swapped, blocks[count:], total)


def solution(mesh):
    occ, vir = mesh.shape["occ"], mesh.shape["vir"]

    def whole(*args):
        return body(*args, occ, vir)

    placed = (P("occ", "vir"), P(None, "vir"), P(), P(), P("occ"))
    return jax.shard_map(
        whole, mesh=mesh, in_specs=placed, out_specs=P("occ", "vir"), check_vma=False
    )
```
